32 devices in a mesh: groups: 2 (over x), dp: 8 (over z, y), tensor: 2 (over core).
Axes of the slice: x: 2, y: 2, z: 4, core: 2. Of those that a mesh axis runs over, the one named last changes fastest.
Arguments:
- x_in: bfloat16 [1536, 8192], P(('groups', 'dp'), 'tensor'), parts along dimension 0, may hold values from -6 to 6
- gate_pre: bfloat16 [1536, 28672], P(('groups', 'dp'), 'tensor'), parts along dimension 0, may hold values from -6 to 6
- up_pre: bfloat16 [1536, 28672], P(('groups', 'dp'), 'tensor'), parts along dimension 0, may hold values from -6 to 6
- grad_hidden: bfloat16 [1536, 28672], P(('groups', 'dp'), 'tensor'), parts along dimension 0, may hold values from -6 to 6
- grad_out: bfloat16 [1536, 8192], P(('groups', 'dp'), 'tensor'), parts along dimension 0, may hold values from -6 to 6
- proj_model: bfloat16 [64, 8192], P('dp', 'tensor'), may hold values from -0.0625 to 0.0625
- proj_hidden: bfloat16 [64, 28672], P('dp', 'tensor'), may hold values from -0.03125 to 0.03125
- lengths: int32 [8], P('groups'), parts along dimension 0, may hold values from 1 to 384, 768 in all
- queries: bfloat16 [512, 12288], P(('groups', 'dp'), 'tensor'), parts along dimension 0, may hold values from -0.0546875 to 0.0546875
- cand: int32 [8, 8], P('groups'), parts along dimension 0, may hold values from 0 to 7
- cand_count: int32 [8], P('groups'), parts along dimension 0, may hold values from 1 to 8
Outputs:
- scores: float32 [8, 8, 32], P('groups'), parts along dimension 0
The draws below stay inside these ranges and needn't reach their ends.
There are 2 independent parts, one for each index of `groups`. The reference program is written for one: setup_inputs(seed, part) draws one part's arguments, and reference() takes and returns one part's arrays. A program takes and returns all parts, laid end to end along the dimension named above; an argument that names none is the same for every part. Nothing has to cross between parts.
Inputs may be any that keep to these rules, and one draw needn't show every extreme that they name: The lengths sum to 768; sequence s occupies the tokens that follow those of sequences 0 to s - 1.
All inputs are finite; a program needn't handle non-finite values.
Results may differ from the reference program's by a relative error of at most 0.0042.
Values may be sent and summed in bfloat16 or wider, within the bound.
No kernel may reach another device: no remote copies, remote signals or barrier semaphores. Data moves between devices by JAX's collectives and lax.ppermute only.
A program may use at most 64 MiB of HBM per device.

```python
import math
import jax
import jax.numpy as jnp
import numpy as np
from jax import lax

D = 8192
FF = 28672
RANK = 64
TOK_DEV = 96
SEQS = 4
QBS = 32
CAND = 8
TOKENS = 768
MOST = 384
QB = 8
QUERIES = 256


def place_ends(values, key, least, high):
    longest = values.shape.index(max(values.shape))
    spots = []
    for shift in (0, 1):
        where = [jax.random.randint(jax.random.fold_in(key, axis), (), 0, length) for axis, length in enumerate(values.shape)]
        where[longest] = (where[longest] + shift) % values.shape[longest]
        spots.append(tuple(where))
    return values.at[spots[0]].set(least).at[spots[1]].set(high)


def level_of(stream_key, shape, pieces, smallest, top_value):
    factor_of, own = 1.0, jax.random.fold_in(stream_key, 6)
    for dim, blocks in pieces:
        draws = jnp.exp(jax.random.uniform(jax.random.fold_in(own, dim), (blocks,), jnp.float32, smallest / len(pieces), top_value / len(pieces)))
        factor_of = factor_of * jnp.repeat(draws, shape[dim] // blocks).reshape([-1 if axis == dim else 1 for axis in range(len(shape))])
    return factor_of


def split_up(amount, total, bound, skew):
    weights = [(1 << 20) // math.isqrt(standing ** skew) + 1 for standing in range(2, amount + 1)]
    surplus, holding = total - bound - (amount - 1), [1] * (amount - 1)
    while surplus > 0:
        movable = [i for i in range(amount - 1) if holding[i] < bound]
        mass, left = sum([weights[i] for i in movable]), surplus
        for i in movable:
            extra = min(bound - holding[i], max(1, left * weights[i] // mass), surplus)
            holding[i] = holding[i] + extra
            surplus = surplus - extra
    return np.array([bound] + holding)


def ragged_sizes(own_key, amount, total, bound, slope):
    if amount == 2:
        one = jax.random.randint(own_key, (), max(1, total - bound), min(bound, total - 1) + 1)
        return jnp.stack([one, total - one])
    sizes = jnp.asarray(split_up(amount, total, bound, slope), jnp.int32)
    twos = (amount - 1) // 2
    source_of, receiver = sizes[1:1 + 2 * twos:2], sizes[2:2 + 2 * twos:2]
    margin = jnp.minimum(source_of - 1, bound - receiver)
    passed = jax.random.randint(jax.random.fold_in(own_key, 1), (twos,), 0, 1 << 20) % (margin + 1)
    sizes = sizes.at[1:1 + 2 * twos:2].set(source_of - passed).at[2:2 + 2 * twos:2].set(receiver + passed)
    return sizes[jax.random.permutation(jax.random.fold_in(own_key, 2), amount)]


def centred(own_key, extent, spread, bound, shards=(), held_as=jnp.bfloat16):
    array = jax.random.normal(own_key, extent, jnp.float32) * spread
    if len(shards) > 0:
        array = level_of(own_key, extent, shards, -0.22, 0.18) * array
    return jnp.clip(array, min=-bound, max=bound).astype(held_as)


def setup_inputs(seed: int = 0, part: int = 0) -> dict:
    streams_of = jax.random.split(jax.random.key(seed), 12)
    part_keys = jax.random.split(jax.random.fold_in(streams_of[11], part), 12)
    x_in = centred(part_keys[0], (TOKENS, D), 1.0, 6.0, ((0, 8), (1, 2)))
    gate_pre = centred(part_keys[1], (TOKENS, FF), 1.0, 6.0, ((0, 8), (1, 2)))
    up_pre = centred(part_keys[2], (TOKENS, FF), 1.0, 6.0, ((0, 8), (1, 2)))
    grad_hidden = centred(part_keys[3], (TOKENS, FF), 1.0, 6.0, ((0, 8), (1, 2)))
    grad_out = centred(part_keys[4], (TOKENS, D), 1.0, 6.0, ((0, 8), (1, 2)))
    proj_model = centred(streams_of[5], (RANK, D), D ** -0.5, 0.0625, ((0, 8), (1, 2)))
    proj_hidden = centred(streams_of[6], (RANK, FF), FF ** -0.5, 0.03125, ((0, 8), (1, 2)))
    lengths = ragged_sizes(part_keys[7], SEQS, TOKENS, MOST, 2).astype(jnp.int32)
    queries = centred(part_keys[8], (QUERIES, 3 * RANK * RANK), (3 * RANK * RANK) ** -0.5, 0.0546875, ((0, 8), (1, 2)))
    cand = place_ends(jax.random.randint(part_keys[9], (SEQS, CAND), 0, QB), jax.random.fold_in(part_keys[9], 1), 0, QB - 1).astype(jnp.int32)
    cand_count = place_ends(jax.random.randint(part_keys[10], (SEQS,), 1, CAND + 1), jax.random.fold_in(part_keys[10], 1), 1, CAND).astype(jnp.int32)
    return dict(x_in=x_in, gate_pre=gate_pre, up_pre=up_pre, grad_hidden=grad_hidden, grad_out=grad_out, proj_model=proj_model, proj_hidden=proj_hidden, lengths=lengths, queries=queries, cand=cand, cand_count=cand_count)


def contract_rows(left, right):
    return lax.dot_general(left, right, (((1,), (1,)), ((), ())), preferred_element_type=jnp.float32)

def reference(x_in, gate_pre, up_pre, grad_hidden, grad_out, proj_model, proj_hidden, lengths, queries, cand, cand_count):

    def project(inputs):
        x_blk, gate_blk, up_blk, grad_blk, out_blk = inputs
        gate_f = gate_blk.astype(jnp.float32)
        up_f = up_blk.astype(jnp.float32)
        grad_f = grad_blk.astype(jnp.float32)
        sig_gate = jax.nn.sigmoid(gate_f)
        hidden_act = (gate_f * sig_gate * up_f).astype(jnp.bfloat16)
        grad_gate = (grad_f * up_f * sig_gate * (1.0 + gate_f * (1.0 - sig_gate))).astype(jnp.bfloat16)
        grad_up = (grad_f * gate_f * sig_gate).astype(jnp.bfloat16)
        return (contract_rows(x_blk, proj_model), contract_rows(hidden_act, proj_hidden), contract_rows(grad_gate, proj_hidden), contract_rows(grad_up, proj_hidden), contract_rows(out_blk, proj_model))
    blocks_n = TOKENS // TOK_DEV

    def split(arr):
        return arr.reshape(blocks_n, TOK_DEV, arr.shape[1])
    outs_all = lax.map(project, (split(x_in), split(gate_pre), split(up_pre), split(grad_hidden), split(grad_out)))
    model_proj, hidden_proj, gate_proj, up_proj, out_proj = [o.reshape(TOKENS, RANK) for o in outs_all]
    position = jnp.arange(TOKENS, dtype=jnp.int32)
    seq_ends = jnp.cumsum(lengths).astype(jnp.int32)
    seq_of = lax.optimization_barrier(jnp.sum((seq_ends[None, :] <= position[:, None]).astype(jnp.int32), axis=1))
    onehot = (seq_of[:, None] == jnp.arange(SEQS, dtype=jnp.int32)[None, :]).astype(jnp.float32)

    def gram_sum(out_vecs, in_vecs):
        left = (onehot[:, :, None] * out_vecs[:, None, :]).reshape(TOKENS, SEQS * RANK)
        return jnp.dot(left.T, in_vecs, precision=lax.Precision.HIGHEST).reshape(SEQS, RANK, RANK)
    seq_grads = jnp.stack([gram_sum(gate_proj, model_proj), gram_sum(up_proj, model_proj), gram_sum(out_proj, hidden_proj)], axis=2)
    seq_grads = seq_grads.reshape(SEQS, 3 * RANK * RANK).astype(jnp.bfloat16)
    full = contract_rows(seq_grads, queries)
    full = full / jnp.sqrt(lengths.astype(jnp.float32))[:, None]
    blocks = full.reshape(SEQS, QB, QBS)
    chosen = jnp.take_along_axis(blocks, cand[:, :, None], axis=1)
    in_use = jnp.arange(CAND, dtype=jnp.int32)[None, :] < cand_count[:, None]
    return jnp.where(in_use[:, :, None], chosen, jnp.float32(0.0))
```

```python
import jax
import jax.numpy as jnp
from jax import lax
from jax.sharding import PartitionSpec as P

QBS = 32
CAND = 8


def contract_rows(left, right):
    return lax.dot_general(
        left, right, (((1,), (1,)), ((), ())), preferred_element_type=jnp.float32
    )


def partner(value, axis, distance):
    size = lax.axis_size(axis)
    return lax.ppermute(value, axis, [(i, i ^ distance) for i in range(size)])


def gather_rows(rows, own):
    size = lax.axis_size("dp")
    pieces = {0: rows}
    for distance in range(2, size, 2):
        pieces[distance] = partner(rows, "dp", distance)
    if size > 1:
        for distance in range(0, size, 2):
            pieces[distance + 1] = partner(pieces[distance], "dp", 1)
    count = rows.shape[0]
    whole = jnp.zeros((size * count, rows.shape[1]), rows.dtype)
    for distance, piece in pieces.items():
        whole = lax.dynamic_update_slice(whole, piece, ((own ^ distance) * count, 0))
    return whole


def double_up(value):
    size = lax.axis_size("dp")
    order = [0]
    distance = size // 2
    while distance:
        value = jnp.concatenate([value, partner(value, "dp", distance)], axis=0)
        order = order + [k ^ distance for k in order]
        distance //= 2
    return value, order


def local(
    x_in,
    gate_pre,
    up_pre,
    grad_hidden,
    grad_out,
    proj_model,
    proj_hidden,
    lengths,
    queries,
    cand,
    cand_count,
):
    own = lax.axis_index("dp")
    core = lax.axis_index("tensor")
    model_width = proj_model.shape[1]
    both = gather_rows(jnp.concatenate([proj_model, proj_hidden], axis=1), own)
    model_rows = both[:, :model_width]
    hidden_rows = both[:, model_width:]
    gate_f = gate_pre.astype(jnp.float32)
    up_f = up_pre.astype(jnp.float32)
    grad_f = grad_hidden.astype(jnp.float32)
    sig_gate = jax.nn.sigmoid(gate_f)
    hidden_act = (gate_f * sig_gate * up_f).astype(jnp.bfloat16)
    grad_gate = (grad_f * up_f * sig_gate * (1.0 + gate_f * (1.0 - sig_gate))).astype(jnp.bfloat16)
    grad_up = (grad_f * gate_f * sig_gate).astype(jnp.bfloat16)
    model_part = contract_rows(x_in, model_rows)
    out_part = contract_rows(grad_out, model_rows)
    hidden_part = contract_rows(hidden_act, hidden_rows)
    gate_part = contract_rows(grad_gate, hidden_rows)
    up_part = contract_rows(grad_up, hidden_rows)
    rank_size = model_part.shape[1]
    half = rank_size // lax.axis_size("tensor")

    def pack(which):
        rows = [
            lax.dynamic_slice_in_dim(p, which * half, half, 1)
            for p in (gate_part, up_part, out_part)
        ]
        return jnp.concatenate(rows + [model_part, hidden_part], axis=1)

    vectors = pack(core) + partner(pack(1 - core), "tensor", 1)
    tok_count = x_in.shape[0]
    tokens, order = double_up(vectors.astype(jnp.bfloat16)[None])
    seq_count = lengths.shape[0]
    owners = jnp.stack([own ^ k for k in order])
    position = owners[:, None] * tok_count + jnp.arange(tok_count, dtype=jnp.int32)[None, :]
    seq_ends = jnp.cumsum(lengths)
    seq_of = jnp.sum((seq_ends[:, None, None] <= position[None]).astype(jnp.int32), axis=0)
    onehot = seq_of[:, :, None] == jnp.arange(seq_count, dtype=jnp.int32)[None, None, :]
    tokens = tokens.reshape(-1, tokens.shape[-1])
    onehot = onehot.reshape(-1, seq_count)
    model_vecs = tokens[:, 3 * half : 3 * half + rank_size]
    hidden_vecs = tokens[:, 3 * half + rank_size :]

    def gram_sum(out_vecs, in_vecs):
        left = jnp.where(onehot[:, :, None], out_vecs[:, None, :], jnp.bfloat16(0)).reshape(
            -1, seq_count * half
        )
        return lax.dot_general(
            left, in_vecs, (((0,), (0,)), ((), ())), preferred_element_type=jnp.float32
        ).reshape(seq_count, half, rank_size)

    grads = jnp.stack(
        [
            gram_sum(tokens[:, :half], model_vecs),
            gram_sum(tokens[:, half : 2 * half], model_vecs),
            gram_sum(tokens[:, 2 * half : 3 * half], hidden_vecs),
        ],
        axis=2,
    )
    grads = grads.reshape(seq_count, half * 3 * rank_size).astype(jnp.bfloat16)
    scores = contract_rows(grads, queries)
    scores = scores + partner(scores, "tensor", 1)
    gathered, order = double_up(scores[None])
    scale = jnp.sqrt(lengths.astype(jnp.float32))[:, None, None]
    per_device = queries.shape[0] // QBS
    blocks = gathered.reshape(len(order), seq_count, per_device, QBS)
    chosen = jnp.zeros((seq_count, CAND, QBS), jnp.float32)
    for k, distance in enumerate(order):
        for j in range(per_device):
            hit = cand == (own ^ distance) * per_device + j
            chosen = jnp.where(hit[:, :, None], blocks[k, :, j][:, None, :], chosen)
    in_use = jnp.arange(CAND, dtype=jnp.int32)[None, :] < cand_count[:, None]
    return jnp.where(in_use[:, :, None], chosen / scale, jnp.float32(0.0))


def solution(mesh):
    placed = (
        P(("groups", "dp"), "tensor"),
        P(("groups", "dp"), "tensor"),
        P(("groups", "dp"), "tensor"),
        P(("groups", "dp"), "tensor"),
        P(("groups", "dp"), "tensor"),
        P("dp", "tensor"),
        P("dp", "tensor"),
        P("groups"),
        P(("groups", "dp"), "tensor"),
        P("groups", None),
        P("groups"),
    )
    return jax.shard_map(
        local, mesh=mesh, in_specs=placed, out_specs=P("groups", None, None), check_vma=False
    )
```

```python
import functools

import jax
import jax.numpy as jnp
from jax import lax
from jax.experimental import pallas as pl
from jax.experimental.pallas import tpu as pltpu
from jax.sharding import PartitionSpec as P

QBS = 32
CAND = 8


def contract_rows(left, right, precision=None):
    return lax.dot_general(
        left,
        right,
        (((1,), (1,)), ((), ())),
        precision=precision,
        preferred_element_type=jnp.float32,
    )


def partner(value, axis, distance):
    size = lax.axis_size(axis)
    return lax.ppermute(value, axis, [(i, i ^ distance) for i in range(size)])


def distances():
    size = lax.axis_size("dp")
    return [1 << k for k in range(size.bit_length() - 1)]


def gather_rows(rows, own):
    size = lax.axis_size("dp")
    pieces = {0: rows}
    for distance in range(2, size, 2):
        pieces[distance] = partner(rows, "dp", distance)
    if size > 1:
        for distance in range(0, size, 2):
            pieces[distance + 1] = partner(pieces[distance], "dp", 1)
    count = rows.shape[0]
    whole = jnp.zeros((size * count, rows.shape[1]), rows.dtype)
    for distance, piece in pieces.items():
        whole = lax.dynamic_update_slice(whole, piece, ((own ^ distance) * count, 0))
    return whole


def halves_of(value, own, distance, dim):
    low, high = jnp.split(value, 2, axis=dim)
    upper = (own & distance) != 0
    return jnp.where(upper, high, low), jnp.where(upper, low, high)


def exchange_queries(queries, own):
    size = lax.axis_size("dp")
    count, width = queries.shape
    value = queries.reshape(count, size, width // size).transpose(1, 0, 2)[None]
    order = [0]
    for distance in distances():
        keep, send = halves_of(value, own, distance, 1)
        value = jnp.concatenate([keep, partner(send, "dp", distance)], axis=0)
        order = order + [k ^ distance for k in order]
    whole = jnp.zeros((size * count, width // size), queries.dtype)
    for k, source in enumerate(order):
        whole = lax.dynamic_update_slice(whole, value[k, 0], ((own ^ source) * count, 0))
    return whole


def act_kernel(gate_ref, up_ref, grad_ref, hidden_out, gate_out, up_out):
    gate = gate_ref[...].astype(jnp.float32)
    up = up_ref[...].astype(jnp.float32)
    grad = grad_ref[...].astype(jnp.float32)
    sig = jax.nn.sigmoid(gate)
    hidden_out[...] = (gate * sig * up).astype(jnp.bfloat16)
    gate_out[...] = (grad * up * sig * (1.0 + gate * (1.0 - sig))).astype(jnp.bfloat16)
    up_out[...] = (grad * gate * sig).astype(jnp.bfloat16)


def activations(gate_pre, up_pre, grad_hidden):
    tokens, width = gate_pre.shape
    block = next(b for b in (2048, 1024, 512, 256, 128, width) if width % b == 0)
    spec = pl.BlockSpec((tokens, block), lambda k: (0, k))
    return pl.pallas_call(
        act_kernel,
        grid=(width // block,),
        in_specs=[spec] * 3,
        out_specs=[spec] * 3,
        out_shape=[jax.ShapeDtypeStruct(gate_pre.shape, jnp.bfloat16)] * 3,
        cost_estimate=pl.CostEstimate(
            flops=12 * tokens * width, transcendentals=tokens * width, bytes_accessed=12 * tokens * width
        ),
        name="activations",
    )(gate_pre, up_pre, grad_hidden)


def gram_kernel(half, rank, lanes, first_ref, lengths_ref, mine_ref, theirs_ref, out_ref):
    vectors = mine_ref[...] + theirs_ref[...]
    tokens, width = vectors.shape
    seq_count = lengths_ref.shape[0]
    groups = half // lanes
    position = first_ref[0] + lax.broadcasted_iota(jnp.int32, (tokens, groups * seq_count), 0)
    slot = lax.broadcasted_iota(jnp.int32, (tokens, groups * seq_count), 1)
    sequence = slot - slot // seq_count * seq_count
    end = jnp.int32(0)
    inside = jnp.zeros((tokens, groups * seq_count), jnp.bool_)
    for s in range(seq_count):
        begin, end = end, end + lengths_ref[s]
        inside = inside | ((sequence == s) & (position >= begin) & (position < end))
    source = lax.broadcasted_iota(jnp.int32, (width, groups * seq_count), 0)
    group = lax.broadcasted_iota(jnp.int32, (width, groups * seq_count), 1) // seq_count
    model_vecs = vectors[:, :rank]
    hidden_vecs = vectors[:, rank : 2 * rank]
    for lane in range(lanes):
        for m in range(3):
            pick = (source == 2 * rank + m * half + group * lanes + lane).astype(jnp.float32)
            spread = lax.dot_general(
                vectors,
                pick,
                (((1,), (0,)), ((), ())),
                precision=lax.Precision.HIGHEST,
                preferred_element_type=jnp.float32,
            )
            left = jnp.where(inside, spread, 0.0)
            product = lax.dot_general(
                left,
                hidden_vecs if m == 2 else model_vecs,
                (((0,), (0,)), ((), ())),
                precision=lax.Precision.HIGHEST,
                preferred_element_type=jnp.float32,
            )
            column = (lane * 3 + m) * rank
            out_ref[:, column : column + rank] = product


def score_kernel(seq_count, mine_ref, theirs_ref, queries_ref, out_ref):
    slices = (mine_ref[...] + theirs_ref[...]).astype(jnp.bfloat16)
    rows, width = slices.shape
    total = None
    for g in range(rows // seq_count):
        part = contract_rows(slices, queries_ref[:, g * width : (g + 1) * width])
        part = part[g * seq_count : (g + 1) * seq_count]
        total = part if total is None else total + part
    out_ref[...] = total


def local(
    x_in,
    gate_pre,
    up_pre,
    grad_hidden,
    grad_out,
    proj_model,
    proj_hidden,
    lengths,
    queries,
    cand,
    cand_count,
):
    size = lax.axis_size("dp")
    own = lax.axis_index("dp")
    core = lax.axis_index("tensor")
    model_width = proj_model.shape[1]
    tok_count = x_in.shape[0]
    seq_count = lengths.shape[0]
    both = gather_rows(jnp.concatenate([proj_model, proj_hidden], axis=1), own)
    query_slice = exchange_queries(queries, own)
    hidden_act, grad_gate, grad_up = activations(gate_pre, up_pre, grad_hidden)
    model_rows = both[:, :model_width]
    hidden_rows = both[:, model_width:]
    model_part = contract_rows(x_in, model_rows)
    out_part = contract_rows(grad_out, model_rows)
    hidden_part = contract_rows(hidden_act, hidden_rows)
    gate_part = contract_rows(grad_gate, hidden_rows)
    up_part = contract_rows(grad_up, hidden_rows)
    rank = model_part.shape[1]
    half = rank // lax.axis_size("tensor")

    def pack(which):
        rows = [
            lax.dynamic_slice_in_dim(p, which * half, half, 1)
            for p in (gate_part, up_part, out_part)
        ]
        return jnp.concatenate([model_part, hidden_part] + rows, axis=1)

    mine = pack(core)
    theirs = partner(pack(1 - core), "tensor", 1)
    lanes = 2 if (half // size) % 2 == 0 else 1
    vmem = pl.BlockSpec(memory_space=pltpu.VMEM)
    smem = pl.BlockSpec(memory_space=pltpu.SMEM)
    grads = pl.pallas_call(
        functools.partial(gram_kernel, half, rank, lanes),
        in_specs=[smem, smem, vmem, vmem],
        out_specs=vmem,
        out_shape=jax.ShapeDtypeStruct(
            (half // lanes * seq_count, lanes * 3 * rank), jnp.float32
        ),
        name="gram",
    )((own * tok_count).astype(jnp.int32)[None], lengths, mine, theirs)
    kept, arrived = grads, None
    for distance in distances():
        if arrived is not None:
            kept = kept + arrived
        kept, sent = halves_of(kept, own, distance, 0)
        arrived = partner(sent, "dp", distance)
    scores = pl.pallas_call(
        functools.partial(score_kernel, seq_count),
        in_specs=[vmem] * 3,
        out_specs=vmem,
        out_shape=jax.ShapeDtypeStruct((seq_count, query_slice.shape[0]), jnp.float32),
        name="score",
    )(kept, arrived, query_slice)
    scores = scores + partner(scores, "tensor", 1)
    for distance in distances():
        scores = scores + partner(scores, "dp", distance)
    scale = jnp.sqrt(lengths.astype(jnp.float32))[:, None, None]
    blocks = scores.reshape(seq_count, -1, QBS)
    chosen = jnp.zeros((seq_count, CAND, QBS), jnp.float32)
    for k in range(blocks.shape[1]):
        chosen = jnp.where((cand == k)[:, :, None], blocks[:, k][:, None, :], chosen)
    in_use = jnp.arange(CAND, dtype=jnp.int32)[None, :] < cand_count[:, None]
    return jnp.where(in_use[:, :, None], chosen / scale, jnp.float32(0.0))


def solution(mesh):
    placed = (
        P(("groups", "dp"), "tensor"),
        P(("groups", "dp"), "tensor"),
        P(("groups", "dp"), "tensor"),
        P(("groups", "dp"), "tensor"),
        P(("groups", "dp"), "tensor"),
        P("dp", "tensor"),
        P("dp", "tensor"),
        P("groups"),
        P(("groups", "dp"), "tensor"),
        P("groups", None),
        P("groups"),
    )
    return jax.shard_map(
        local, mesh=mesh, in_specs=placed, out_specs=P("groups", None, None), check_vma=False
    )
```

```python
import functools

import jax
import jax.numpy as jnp
from jax import lax
from jax.experimental import pallas as pl
from jax.experimental.pallas import tpu as pltpu
from jax.sharding import PartitionSpec as P

QBS = 32
CAND = 8


def contract_rows(left, right, precision=None):
    return lax.dot_general(
        left,
        right,
        (((1,), (1,)), ((), ())),
        precision=precision,
        preferred_element_type=jnp.float32,
    )


def partner(value, axis, distance):
    size = lax.axis_size(axis)
    return lax.ppermute(value, axis, [(i, i ^ distance) for i in range(size)])


def distances():
    size = lax.axis_size("dp")
    return [1 << k for k in range(size.bit_length() - 1)]


def gather_rows(rows, own):
    size = lax.axis_size("dp")
    pieces = {0: rows}
    for distance in range(2, size, 2):
        pieces[distance] = partner(rows, "dp", distance)
    if size > 1:
        for distance in range(0, size, 2):
            pieces[distance + 1] = partner(pieces[distance], "dp", 1)
    count = rows.shape[0]
    whole = jnp.zeros((size * count, rows.shape[1]), rows.dtype)
    for distance, piece in pieces.items():
        whole = lax.dynamic_update_slice(whole, piece, ((own ^ distance) * count, 0))
    return whole


def halves_of(value, own, distance, dim):
    low, high = jnp.split(value, 2, axis=dim)
    upper = (own & distance) != 0
    return jnp.where(upper, high, low), jnp.where(upper, low, high)


def exchange_queries(queries, own):
    size = lax.axis_size("dp")
    count, width = queries.shape
    value = queries.reshape(count, size, width // size).transpose(1, 0, 2)[None]
    order = [0]
    for distance in distances():
        keep, send = halves_of(value, own, distance, 1)
        value = jnp.concatenate([keep, partner(send, "dp", distance)], axis=0)
        order = order + [k ^ distance for k in order]
    whole = jnp.zeros((size * count, width // size), queries.dtype)
    for k, source in enumerate(order):
        whole = lax.dynamic_update_slice(whole, value[k, 0], ((own ^ source) * count, 0))
    return whole


def act_kernel(tokens, gate_ref, up_ref, grad_ref, out_ref):
    gate = gate_ref[...].astype(jnp.float32)
    up = up_ref[...].astype(jnp.float32)
    grad = grad_ref[...].astype(jnp.float32)
    sig = jax.nn.sigmoid(gate)
    out_ref[:tokens] = (gate * sig * up).astype(jnp.bfloat16)
    slope = sig * (1.0 + gate * (1.0 - sig))
    out_ref[tokens : 2 * tokens] = (grad * up * slope).astype(jnp.bfloat16)
    out_ref[2 * tokens :] = (grad * gate * sig).astype(jnp.bfloat16)


def activations(gate_pre, up_pre, grad_hidden):
    tokens, width = gate_pre.shape
    block = next(b for b in (2048, 1024, 512, 256, 128, width) if width % b == 0)
    spec = pl.BlockSpec((tokens, block), lambda k: (0, k))
    return pl.pallas_call(
        functools.partial(act_kernel, tokens),
        grid=(width // block,),
        in_specs=[spec] * 3,
        out_specs=pl.BlockSpec((3 * tokens, block), lambda k: (0, k)),
        out_shape=jax.ShapeDtypeStruct((3 * tokens, width), jnp.bfloat16),
        cost_estimate=pl.CostEstimate(
            flops=20 * tokens * width, transcendentals=tokens * width, bytes_accessed=12 * tokens * width
        ),
        compiler_params=pltpu.CompilerParams(vmem_limit_bytes=12 << 20),
        name="activations",
    )(gate_pre, up_pre, grad_hidden)


def project_kernel(core_ref, acts_ref, x_ref, grad_ref, rows_ref, mine_ref, send_ref):
    tokens, model_width = x_ref.shape
    width = acts_ref.shape[1]
    rank = rows_ref.shape[0]
    chunk = next(b for b in (2048, 1024, 512, 256, 128, width) if width % b == 0)

    def step(k, total):
        at = pl.multiple_of(k * chunk, chunk)
        return total + contract_rows(
            acts_ref[:, pl.ds(at, chunk)], rows_ref[:, pl.ds(model_width + at, chunk)]
        )

    total = lax.fori_loop(
        0, width // chunk, step, jnp.zeros((3 * tokens, rank), jnp.float32)
    )
    model_rows = rows_ref[:, :model_width]
    model_vecs = contract_rows(x_ref[...], model_rows)
    out_vecs = contract_rows(grad_ref[...], model_rows)
    hidden_vecs = total[:tokens]
    half = rank // 2
    lower = core_ref[0] == 0
    for ref in (mine_ref, send_ref):
        ref[:, :rank] = model_vecs
        ref[:, rank : 2 * rank] = hidden_vecs
    column = 2 * rank
    for vecs in (total[tokens : 2 * tokens], total[2 * tokens :], out_vecs):
        left, right = vecs[:, :half], vecs[:, half:]
        mine_ref[:, column : column + half] = jnp.where(lower, left, right)
        send_ref[:, column : column + half] = jnp.where(lower, right, left)
        column += half


def gram_kernel(half, rank, first_ref, lengths_ref, mine_ref, theirs_ref, out_ref):
    vectors = mine_ref[...] + theirs_ref[...]
    tokens = vectors.shape[0]
    seq_count = lengths_ref.shape[0]
    position = first_ref[0] + lax.broadcasted_iota(jnp.int32, (tokens, rank), 0)
    model_vecs, hidden_vecs = vectors[:, :rank], vectors[:, rank : 2 * rank]
    end = jnp.int32(0)
    masked = []
    for s in range(seq_count):
        begin, end = end, end + lengths_ref[s]
        inside = (position >= begin) & (position < end)
        masked.append((jnp.where(inside, model_vecs, 0.0), jnp.where(inside, hidden_vecs, 0.0)))

    def product(left, which):
        return lax.dot_general(
            left,
            jnp.concatenate([pair[which] for pair in masked], axis=1),
            (((0,), (0,)), ((), ())),
            precision=lax.Precision.HIGHEST,
            preferred_element_type=jnp.float32,
        )

    with_model = product(vectors[:, 2 * rank : 2 * rank + 2 * half], 0)
    with_hidden = product(vectors[:, 2 * rank + 2 * half : 2 * rank + 3 * half], 1)
    for s in range(seq_count):
        at = slice(s * rank, (s + 1) * rank)
        out_ref[:, 3 * s * rank : 3 * (s + 1) * rank] = jnp.concatenate(
            [with_model[:half, at], with_model[half:, at], with_hidden[:, at]], axis=1
        )


def score_kernel(seq_count, mine_ref, theirs_ref, queries_ref, out_ref):
    slices = mine_ref[...] + theirs_ref[...]
    rows = slices.shape[0]
    width = slices.shape[1] // seq_count
    flat = jnp.concatenate(
        [
            jnp.concatenate(
                [slices[i : i + 1, s * width : (s + 1) * width] for i in range(rows)], axis=1
            )
            for s in range(seq_count)
        ],
        axis=0,
    )
    out_ref[...] = contract_rows(flat.astype(jnp.bfloat16), queries_ref[...])


def local(
    x_in,
    gate_pre,
    up_pre,
    grad_hidden,
    grad_out,
    proj_model,
    proj_hidden,
    lengths,
    queries,
    cand,
    cand_count,
):
    own = lax.axis_index("dp")
    core = lax.axis_index("tensor")
    tok_count = x_in.shape[0]
    seq_count = lengths.shape[0]
    both = gather_rows(jnp.concatenate([proj_model, proj_hidden], axis=1), own)
    query_slice = exchange_queries(queries, own)
    acts = activations(gate_pre, up_pre, grad_hidden)
    rank = both.shape[0]
    half = rank // lax.axis_size("tensor")
    packed = 2 * rank + 3 * half
    vmem = pl.BlockSpec(memory_space=pltpu.VMEM)
    smem = pl.BlockSpec(memory_space=pltpu.SMEM)
    mine, send = pl.pallas_call(
        project_kernel,
        in_specs=[smem, vmem, vmem, vmem, vmem],
        out_specs=[vmem, vmem],
        out_shape=[jax.ShapeDtypeStruct((tok_count, packed), jnp.float32)] * 2,
        compiler_params=pltpu.CompilerParams(vmem_limit_bytes=24 << 20),
        name="project",
    )(core.astype(jnp.int32)[None], acts, x_in, grad_out, both)
    theirs = partner(send, "tensor", 1)
    grads = pl.pallas_call(
        functools.partial(gram_kernel, half, rank),
        in_specs=[smem, smem, vmem, vmem],
        out_specs=vmem,
        out_shape=jax.ShapeDtypeStruct((half, seq_count * 3 * rank), jnp.float32),
        compiler_params=pltpu.CompilerParams(vmem_limit_bytes=6 << 20),
        name="gram",
    )((own * tok_count).astype(jnp.int32)[None], lengths, mine, theirs)
    kept, arrived = grads, None
    for distance in distances():
        if arrived is not None:
            kept = kept + arrived
        kept, sent = halves_of(kept, own, distance, 0)
        arrived = partner(sent, "dp", distance)
    scores = pl.pallas_call(
        functools.partial(score_kernel, seq_count),
        in_specs=[vmem] * 3,
        out_specs=vmem,
        out_shape=jax.ShapeDtypeStruct((seq_count, query_slice.shape[0]), jnp.float32),
        compiler_params=pltpu.CompilerParams(vmem_limit_bytes=4 << 20),
        name="score",
    )(kept, arrived, query_slice)
    scores = scores + partner(scores, "tensor", 1)
    for distance in distances():
        scores = scores + partner(scores, "dp", distance)
    scale = jnp.sqrt(lengths.astype(jnp.float32))[:, None, None]
    blocks = scores.reshape(seq_count, -1, QBS)
    chosen = jnp.zeros((seq_count, CAND, QBS), jnp.float32)
    for k in range(blocks.shape[1]):
        chosen = jnp.where((cand == k)[:, :, None], blocks[:, k][:, None, :], chosen)
    in_use = jnp.arange(CAND, dtype=jnp.int32)[None, :] < cand_count[:, None]
    return jnp.where(in_use[:, :, None], chosen / scale, jnp.float32(0.0))


def solution(mesh):
    placed = (
        P(("groups", "dp"), "tensor"),
        P(("groups", "dp"), "tensor"),
        P(("groups", "dp"), "tensor"),
        P(("groups", "dp"), "tensor"),
        P(("groups", "dp"), "tensor"),
        P("dp", "tensor"),
        P("dp", "tensor"),
        P("groups"),
        P(("groups", "dp"), "tensor"),
        P("groups", None),
        P("groups"),
    )
    return jax.shard_map(
        local, mesh=mesh, in_specs=placed, out_specs=P("groups", None, None), check_vma=False
    )
```
